32 devices in a mesh: chan: 4 (over y, core), tm: 8 (over z, x).
Axes of the slice: x: 2, y: 2, z: 4, core: 2. Of those that a mesh axis runs over, the one named last changes fastest.
Arguments:
- readings: float32 [8192, 8192], P('chan', 'tm'), may hold values from -8 to 8
- channel_start: float32 [8192, 64], P(('chan', 'tm')), may hold values from -6 to 6
- time_start: float32 [8192, 64], P(('tm', 'chan')), may hold values from -0.75 to 0.75
Outputs:
- outliers: float32 [8192, 8192], P('chan', 'tm')
- channel_factors: float32 [8192, 64], P(('chan', 'tm'))
- time_factors: float32 [8192, 64], P(('tm', 'chan'))
The draws below stay inside these ranges and needn't reach their ends.
All inputs are finite; a program needn't handle non-finite values.
Results may differ from the reference program's by a relative error of at most 0.00019.
Values sent between devices are 32-bit elements; how exact they have to be, the bound alone decides.
A program may use at most 128 MiB of HBM per device.

```python
import jax
import jax.numpy as jnp
from jax import lax

RANK = 64
ITERS = 2
CHANNELS = 8192
TIMES = 8192


def levels(own_key, shape, pieces, low, top_value):
    factor_of, own = 1.0, jax.random.fold_in(own_key, 6)
    for axis_at, shards_of in pieces:
        heights = jnp.exp(jax.random.uniform(jax.random.fold_in(own, axis_at), (shards_of,), jnp.float32, low / len(pieces), top_value / len(pieces)))
        factor_of = factor_of * jnp.repeat(heights, shape[axis_at] // shards_of).reshape([-1 if axis == axis_at else 1 for axis in range(len(shape))])
    return factor_of


def centred(stream_key, dims, scale, bound, cuts=(), held_as=jnp.bfloat16):
    values = jax.random.normal(stream_key, dims, jnp.float32) * scale
    if len(cuts) > 0:
        values = levels(stream_key, dims, cuts, -0.22, 0.18) * values
    return jnp.clip(values, min=-bound, max=bound).astype(held_as)


def setup_inputs(seed: int = 0) -> dict:
    key_list = jax.random.split(jax.random.key(seed), 4)
    readings = centred(key_list[0], (CHANNELS, TIMES), 1.0, 8.0, ((0, 4), (1, 8)), jnp.float32)
    channel_start = centred(key_list[1], (CHANNELS, RANK), 1.0, 6.0, ((0, 32),), jnp.float32)
    time_start = centred(key_list[2], (TIMES, RANK), RANK ** -0.5, 0.75, ((0, 32),), jnp.float32)
    return dict(readings=readings, channel_start=channel_start, time_start=time_start)


threshold_level = 1.5
ridge_weight = 8.0

def product(first, second):
    return jnp.dot(first.astype(jnp.float32), second.astype(jnp.float32), precision=lax.Precision.HIGHEST, preferred_element_type=jnp.float32)

def solve_ridge(partial_value, gram):
    factor_chol = jnp.linalg.cholesky(gram)
    middle = lax.linalg.triangular_solve(factor_chol, partial_value, left_side=False, lower=True, transpose_a=True)
    return lax.linalg.triangular_solve(factor_chol, middle, left_side=False, lower=True, transpose_a=False)

def reference(readings, channel_start, time_start):
    identity = jnp.eye(RANK, dtype=jnp.float32)
    left_factor = channel_start
    right_factor = time_start
    outliers = readings
    for sweep in range(ITERS):
        residue = readings - product(left_factor, right_factor.T)
        outliers = residue - jnp.clip(residue, -threshold_level, threshold_level)
        cleaned = readings - outliers
        gram_right = product(right_factor.T, right_factor) + ridge_weight * identity
        left_factor = solve_ridge(product(cleaned, right_factor), gram_right)
        gram_left = product(left_factor.T, left_factor) + ridge_weight * identity
        right_factor = solve_ridge(product(cleaned.T, left_factor), gram_left)
    return (outliers, left_factor, right_factor)
```

```python
import functools

import jax
import jax.numpy as jnp
from jax import lax
from jax.experimental import pallas as pl
from jax.experimental.pallas import tpu as pltpu
from jax.sharding import PartitionSpec as P

ITERS = 2
LEVEL = 1.5
RIDGE = 8.0
MESH = pl.DeviceIdType.MESH
HIGHEST = lax.Precision.HIGHEST


def split(value):
    high = value.astype(jnp.bfloat16)
    low = (value - high.astype(jnp.float32)).astype(jnp.bfloat16)
    return high, low


def stacked(value):
    high = value.astype(jnp.bfloat16).astype(jnp.float32)
    return jnp.concatenate([high, value - high], axis=0)


def dot(first, second):
    return jnp.dot(first, second, preferred_element_type=jnp.float32)


def outer_gram(value):
    return lax.dot_general(value, value, (((1,), (1,)), ((), ())), precision=HIGHEST,
                           preferred_element_type=jnp.float32)


def inverse(gram):
    rank = gram.shape[0]
    rows = lax.broadcasted_iota(jnp.int32, (rank, rank), 0)
    cols = lax.broadcasted_iota(jnp.int32, (rank, rank), 1)
    for k in range(rank):
        row = gram[k:k + 1, :]
        col = gram[:, k:k + 1]
        inv = 1.0 / gram[k:k + 1, k:k + 1]
        scaled = jnp.where(cols[:1] == k, 1.0, row) * inv
        rest = jnp.where(cols == k, 0.0, gram) - col * scaled
        gram = jnp.where(rows == k, scaled, rest)
    return gram


def kernel(n, m, x_hbm, l0, r0, out_hbm, lout, rout,
           x, clean, lg, sbuf, srecv, rg, tbuf, trecv, gl, gr, glrecv, grrecv,
           rcat, rwide, acc, inv_r,
           l_s, l_r, s_s, s_r, t_s, t_r, r_s, r_r, gl_s, gl_r, gr_s, gr_r, x_sem, o_sem):
    c = lax.axis_index("chan")
    t = lax.axis_index("tm")
    rank, lc = l0.shape
    rc = r0.shape[1]
    times = x.shape[1]
    width = 256

    def peer_t(s):
        return lax.rem(t + s, n)

    def peer_c(s):
        return lax.rem(c + s, m)

    def copy_t(src, dst, ssem, rsem, j):
        return pltpu.make_async_remote_copy(src_ref=src, dst_ref=dst, send_sem=ssem, recv_sem=rsem,
                                            device_id=(c, j), device_id_type=MESH)

    def copy_c(src, dst, ssem, rsem, j):
        return pltpu.make_async_remote_copy(src_ref=src, dst_ref=dst, send_sem=ssem, recv_sem=rsem,
                                            device_id=(j, t), device_id_type=MESH)

    def loop(first, last, body):
        def step(s, carry):
            body(s)
            return carry
        lax.fori_loop(first, last, step, 0)

    def left_copy(g, j, slot):
        src = l0 if g == 0 else lg.at[g, t]
        return copy_t(src, lg.at[g, slot], l_s.at[g, j], l_r.at[g, slot], j)

    def s_copy(i, j, slot):
        return copy_t(sbuf.at[i, j], srecv.at[i, slot], s_s.at[i, j], s_r.at[i, slot], j)

    def gr_copy(i, j, slot):
        return copy_t(gr.at[i], grrecv.at[i, slot], gr_s.at[i, j], gr_r.at[i, slot], j)

    def right_copy(g, j, slot):
        src = r0 if g == 0 else rg.at[g, c]
        return copy_c(src, rg.at[g, slot], r_s.at[g, j], r_r.at[g, slot], j)

    def t_copy(i, j, slot):
        return copy_c(tbuf.at[i, j], trecv.at[i, slot], t_s.at[i, j], t_r.at[i, slot], j)

    def gl_copy(i, j, slot):
        return copy_c(gl.at[i], glrecv.at[i, slot], gl_s.at[i, j], gl_r.at[i, slot], j)

    def rows_of(j):
        return pl.ds(pl.multiple_of(j * lc, lc), lc)

    def x_copy(j):
        return pltpu.make_async_copy(x_hbm.at[rows_of(j)], x.at[rows_of(j)], x_sem.at[j])

    def o_copy(j):
        return pltpu.make_async_copy(x.at[rows_of(j)], out_hbm.at[rows_of(j)], o_sem.at[j])

    loop(0, n, lambda s: x_copy(peer_t(s)).start())

    barrier = pltpu.get_barrier_semaphore()
    loop(1, n, lambda s: pl.semaphore_signal(barrier, inc=1, device_id=(c, peer_t(s)), device_id_type=MESH))
    loop(1, m, lambda s: pl.semaphore_signal(barrier, inc=1, device_id=(peer_c(s), t), device_id_type=MESH))
    pl.semaphore_wait(barrier, n + m - 2)

    loop(1, m, lambda s: right_copy(0, peer_c(s), c).start())
    loop(1, n, lambda s: left_copy(0, peer_t(s), t).start())
    lg[0, t] = l0[...]
    rg[0, c] = r0[...]

    rows = lax.broadcasted_iota(jnp.int32, (rank, rank), 0)
    cols = lax.broadcasted_iota(jnp.int32, (rank, rank), 1)
    ridge = jnp.where(rows == cols, RIDGE, 0.0).astype(jnp.float32)

    for i in range(ITERS):
        last = i == ITERS - 1

        loop(1, m, lambda s: right_copy(i, c, peer_c(s)).wait_recv())
        total = None
        for q in range(m):
            part = rg[i, q]
            both = stacked(part)
            high = both[:rank]
            low = both[rank:]
            at = pl.ds(q * rc, rc)
            rcat[:, at] = jnp.concatenate([high, high, low, low], axis=0).astype(jnp.bfloat16)
            rwide[at, :] = both.T.astype(jnp.bfloat16)
            term = outer_gram(part)
            total = term if total is None else total + term
        gr[i] = total
        grrecv[i, t] = total
        loop(1, n, lambda s: gr_copy(i, peer_t(s), t).start())

        def block_a(s):
            j = peer_t(s)

            @pl.when(s > 0)
            def _():
                left_copy(i, t, j).wait_recv() if i == 0 else None

            if i == 0:
                x_copy(j).wait()
            two = stacked(lg[i, j]).T.astype(jnp.bfloat16)
            lcat = jnp.concatenate([two, two], axis=1)
            at = rows_of(j)
            sums = jnp.zeros((lc, 2 * rank), jnp.float32)
            for b in range(times // width):
                part = pl.ds(b * width, width)
                values = x[at, part]
                residue = values - dot(lcat, rcat[:, part])
                outlier = residue - jnp.clip(residue, -LEVEL, LEVEL)
                high, low = split(values - outlier)
                if last:
                    x[at, part] = outlier
                clean[0, at, part] = high
                clean[1, at, part] = low
                sums += dot(high, rwide[part, :]) + dot(low, rwide[part, :])
            flat = sums.T
            sbuf[i, j] = flat[:rank] + flat[rank:]
            if last:
                o_copy(j).start()

            @pl.when(s > 0)
            def _():
                s_copy(i, j, t).start()

        loop(0, n, block_a)

        loop(1, n, lambda s: gr_copy(i, t, peer_t(s)).wait_recv())
        total = ridge
        for q in range(n):
            total = total + grrecv[i, q]
        inv_r[...] = inverse(total)

        def add_s(s, value):
            j = lax.rem(t + n - s, n)
            s_copy(i, t, j).wait_recv()
            return value + srecv[i, j]

        total = lax.fori_loop(1, n, add_s, sbuf[i, t])
        piece = jnp.dot(inv_r[...], total, precision=HIGHEST, preferred_element_type=jnp.float32)
        lg[i + 1, t] = piece
        loop(1, n, lambda s: left_copy(i + 1, peer_t(s), t).start())
        if last:
            lout[...] = piece

        acc[...] = jnp.zeros_like(acc)

        def block_b(s, gram):
            j = lax.rem(t + n - s, n)

            @pl.when(s > 0)
            def _():
                left_copy(i + 1, t, j).wait_recv()

            value = lg[i + 1, j]
            both = stacked(value).astype(jnp.bfloat16)
            at = rows_of(j)
            for b in range(times // width):
                part = pl.ds(b * width, width)
                acc[:, part] += dot(both, clean[0, at, part]) + dot(both, clean[1, at, part])
            return gram + outer_gram(value)

        gram = lax.fori_loop(0, n, block_b, jnp.zeros((rank, rank), jnp.float32))
        gl[i] = gram
        glrecv[i, c] = gram
        loop(1, m, lambda s: gl_copy(i, peer_c(s), c).start())
        for q in range(m):
            at = pl.ds(q * rc, rc)
            tbuf[i, q] = acc[:rank, at] + acc[rank:, at]
        loop(1, m, lambda s: t_copy(i, peer_c(s), c).start())
        loop(1, m, lambda s: gl_copy(i, c, peer_c(s)).wait_recv())
        total = ridge
        for q in range(m):
            total = total + glrecv[i, q]
        inv_l = inverse(total)

        def add_t(s, value):
            j = peer_c(s)
            t_copy(i, c, j).wait_recv()
            return value + trecv[i, j]

        total = lax.fori_loop(1, m, add_t, tbuf[i, c])
        piece = jnp.dot(inv_l, total, precision=HIGHEST, preferred_element_type=jnp.float32)
        if last:
            rout[...] = piece
        else:
            rg[i + 1, c] = piece
            loop(1, m, lambda s: right_copy(i + 1, peer_c(s), c).start())

    for i in range(ITERS):
        loop(1, n, lambda s: s_copy(i, peer_t(s), t).wait_send())
        loop(1, n, lambda s: gr_copy(i, peer_t(s), t).wait_send())
        loop(1, m, lambda s: t_copy(i, peer_c(s), c).wait_send())
        loop(1, m, lambda s: gl_copy(i, peer_c(s), c).wait_send())
        loop(1, m, lambda s: right_copy(i, peer_c(s), c).wait_send())
    for i in range(ITERS + 1):
        loop(1, n, lambda s: left_copy(i, peer_t(s), t).wait_send())
    loop(0, n, lambda s: o_copy(peer_t(s)).wait())


def shards(n, m, readings, channel_start, time_start):
    lc, rank = channel_start.shape
    rc = time_start.shape[0]
    rows, times = readings.shape
    f32 = jnp.float32
    vmem = pl.BlockSpec(memory_space=pltpu.VMEM)
    anywhere = pl.BlockSpec(memory_space=pl.ANY)
    dma = pltpu.SemaphoreType.DMA
    outliers, left, right = pl.pallas_call(
        functools.partial(kernel, n, m),
        out_shape=(jax.ShapeDtypeStruct((rows, times), f32),
                   jax.ShapeDtypeStruct((rank, lc), f32),
                   jax.ShapeDtypeStruct((rank, rc), f32)),
        in_specs=[anywhere, vmem, vmem],
        out_specs=(anywhere, vmem, vmem),
        scratch_shapes=[
            pltpu.VMEM((rows, times), f32),
            pltpu.VMEM((2, rows, times), jnp.bfloat16),
            pltpu.VMEM((ITERS + 1, n, rank, lc), f32),
            pltpu.VMEM((ITERS, n, rank, lc), f32),
            pltpu.VMEM((ITERS, n, rank, lc), f32),
            pltpu.VMEM((ITERS, m, rank, rc), f32),
            pltpu.VMEM((ITERS, m, rank, rc), f32),
            pltpu.VMEM((ITERS, m, rank, rc), f32),
            pltpu.VMEM((ITERS, rank, rank), f32),
            pltpu.VMEM((ITERS, rank, rank), f32),
            pltpu.VMEM((ITERS, m, rank, rank), f32),
            pltpu.VMEM((ITERS, n, rank, rank), f32),
            pltpu.VMEM((4 * rank, times), jnp.bfloat16),
            pltpu.VMEM((times, 2 * rank), jnp.bfloat16),
            pltpu.VMEM((2 * rank, times), f32),
            pltpu.VMEM((rank, rank), f32),
            dma((ITERS + 1, n)), dma((ITERS + 1, n)),
            dma((ITERS, n)), dma((ITERS, n)),
            dma((ITERS, m)), dma((ITERS, m)),
            dma((ITERS, m)), dma((ITERS, m)),
            dma((ITERS, m)), dma((ITERS, m)),
            dma((ITERS, n)), dma((ITERS, n)),
            dma((n,)), dma((n,)),
        ],
        compiler_params=pltpu.CompilerParams(collective_id=0, has_side_effects=True,
                                             vmem_limit_bytes=48 * 1024 * 1024),
    )(readings, channel_start.T, time_start.T)
    return outliers, left.T, right.T


def solution(mesh):
    n, m = mesh.shape["tm"], mesh.shape["chan"]
    specs = (P("chan", "tm"), P(("chan", "tm"), None), P(("tm", "chan"), None))
    return jax.shard_map(functools.partial(shards, n, m), mesh=mesh, in_specs=specs, out_specs=specs,
                         check_vma=False)
```

```python
import functools

import jax
import jax.numpy as jnp
from jax import lax
from jax.experimental import pallas as pl
from jax.experimental.pallas import tpu as pltpu
from jax.sharding import PartitionSpec as P

ITERS = 2
LEVEL = 1.5
RIDGE = 8.0
MESH = pl.DeviceIdType.MESH
HIGHEST = lax.Precision.HIGHEST


def split(value):
    high = value.astype(jnp.bfloat16)
    low = (value - high.astype(jnp.float32)).astype(jnp.bfloat16)
    return high, low


def stacked(value):
    high = value.astype(jnp.bfloat16).astype(jnp.float32)
    return jnp.concatenate([high, value - high], axis=0)


def dot(first, second):
    return jnp.dot(first, second, preferred_element_type=jnp.float32)


def outer_gram(value):
    return lax.dot_general(value, value, (((1,), (1,)), ((), ())), precision=HIGHEST,
                           preferred_element_type=jnp.float32)


def inverse(gram):
    rank = gram.shape[0]
    rows = lax.broadcasted_iota(jnp.int32, (rank, rank), 0)
    cols = lax.broadcasted_iota(jnp.int32, (rank, rank), 1)
    lane = cols[:1]
    for k in range(0, rank, 2):
        up, down = gram[k:k + 1, :], gram[k + 1:k + 2, :]
        first, second = gram[:, k:k + 1], gram[:, k + 1:k + 2]
        wide = lambda value: jnp.broadcast_to(value, (1, rank))
        p, q = wide(up[:, k:k + 1]), wide(up[:, k + 1:k + 2])
        r, d = wide(down[:, k:k + 1]), wide(down[:, k + 1:k + 2])
        inv = 1.0 / (p * d - q * r)
        up = jnp.where(lane == k, 1.0, jnp.where(lane == k + 1, 0.0, up))
        down = jnp.where(lane == k, 0.0, jnp.where(lane == k + 1, 1.0, down))
        new_up = (d * up - q * down) * inv
        new_down = (p * down - r * up) * inv
        rest = jnp.where((cols == k) | (cols == k + 1), 0.0, gram) - first * new_up - second * new_down
        gram = jnp.where(rows == k, new_up, jnp.where(rows == k + 1, new_down, rest))
    return gram


def kernel(n, m, x_hbm, l0, r0, x, lout, rout,
           clean, lg, sbuf, precv, srecv, rg, tbuf, trecv, gl, gr, glrecv, grrecv,
           rcat, rwide, acc, inv_r,
           lz_s, lx_s, l_r, p_s, p_r, s_s, s_r, t_s, t_r, r_s, r_r, gl_s, gl_r, gr_s, gr_r, x_sem):
    c = lax.axis_index("chan")
    t = lax.axis_index("tm")
    rank, lc = l0.shape
    rc = r0.shape[1]
    times = x.shape[1]
    width = 256
    half = n // 2
    z, pair = t // 2, t % 2
    other = z * 2 + 1 - pair

    def flip(s):
        value, bit = 0, 1
        while bit < half:
            value = value + bit * ((z // bit + s // bit) % 2)
            bit *= 2
        return value

    def mine(q):
        return q * 2 + pair

    def theirs(q):
        return q * 2 + 1 - pair

    def peer_t(s):
        return lax.rem(t + s, n)

    def peer_c(s):
        return lax.rem(c + s, m)

    def copy_t(src, dst, ssem, rsem, j):
        return pltpu.make_async_remote_copy(src_ref=src, dst_ref=dst, send_sem=ssem, recv_sem=rsem,
                                            device_id=(c, j), device_id_type=MESH)

    def copy_c(src, dst, ssem, rsem, j):
        return pltpu.make_async_remote_copy(src_ref=src, dst_ref=dst, send_sem=ssem, recv_sem=rsem,
                                            device_id=(j, t), device_id_type=MESH)

    def loop(first, last, body):
        def step(s, carry):
            body(s)
            return carry
        lax.fori_loop(first, last, step, 0)

    def left_src(g, q, own):
        return l0 if own and g == 0 else lg.at[g, mine(q)]

    def left_z(g, q, slot, own=True):
        return copy_t(left_src(g, z, own), lg.at[g, slot], lz_s.at[g, q], l_r.at[g, slot], mine(q))

    def left_x(g, q, slot, own):
        return copy_t(left_src(g, q, own), lg.at[g, slot], lx_s.at[g, q], l_r.at[g, slot], other)

    def left_send(g):
        loop(1, half, lambda s: left_z(g, flip(s), t).start())
        left_x(g, z, t, True).start()

    def left_wait(g, q):
        left_z(g, q, mine(q)).wait_recv()
        left_x(g, q, mine(q), False).start()

    def left_wait_other(g, q):
        left_x(g, q, theirs(q), False).wait_recv()

    def pair_copy(i, q, slot):
        return copy_t(sbuf.at[i, theirs(q)], precv.at[i, slot], p_s.at[i, q], p_r.at[i, slot], other)

    def s_copy(i, q, slot):
        return copy_t(sbuf.at[i, mine(q)], srecv.at[i, slot], s_s.at[i, q], s_r.at[i, slot], mine(q))

    def gr_copy(i, j, slot):
        return copy_t(gr.at[i], grrecv.at[i, slot], gr_s.at[i, j], gr_r.at[i, slot], j)

    def right_copy(g, j, slot):
        src = r0 if g == 0 else rg.at[g, c]
        return copy_c(src, rg.at[g, slot], r_s.at[g, j], r_r.at[g, slot], j)

    def t_copy(i, j, slot):
        return copy_c(tbuf.at[i, j], trecv.at[i, slot], t_s.at[i, j], t_r.at[i, slot], j)

    def gl_copy(i, j, slot):
        return copy_c(gl.at[i], glrecv.at[i, slot], gl_s.at[i, j], gl_r.at[i, slot], j)

    def rows_of(j):
        return pl.ds(pl.multiple_of(j * lc, lc), lc)

    def x_copy(j):
        return pltpu.make_async_copy(x_hbm.at[rows_of(j)], x.at[rows_of(j)], x_sem.at[j])

    def first_of(i, s):
        q = flip(s)

        @pl.when(s > 0)
        def _():
            left_wait(i, q)
        return q

    loop(0, half, lambda s: x_copy(mine(flip(s))).start())
    loop(0, half, lambda s: x_copy(theirs(flip(s))).start())

    barrier = pltpu.get_barrier_semaphore()
    loop(1, n, lambda s: pl.semaphore_signal(barrier, inc=1, device_id=(c, peer_t(s)), device_id_type=MESH))
    loop(1, m, lambda s: pl.semaphore_signal(barrier, inc=1, device_id=(peer_c(s), t), device_id_type=MESH))
    pl.semaphore_wait(barrier, n + m - 2)

    loop(1, m, lambda s: right_copy(0, peer_c(s), c).start())
    left_send(0)
    lg[0, t] = l0[...]
    rg[0, c] = r0[...]

    rows = lax.broadcasted_iota(jnp.int32, (rank, rank), 0)
    cols = lax.broadcasted_iota(jnp.int32, (rank, rank), 1)
    ridge = jnp.where(rows == cols, RIDGE, 0.0).astype(jnp.float32)

    for i in range(ITERS):
        last = i == ITERS - 1

        loop(1, m, lambda s: right_copy(i, c, peer_c(s)).wait_recv())
        total = None
        for q in range(m):
            part = rg[i, q]
            both = stacked(part)
            high = both[:rank]
            low = both[rank:]
            at = pl.ds(q * rc, rc)
            rcat[:, at] = jnp.concatenate([high, high, low, low], axis=0).astype(jnp.bfloat16)
            rwide[at, :] = both.T.astype(jnp.bfloat16)
            term = outer_gram(part)
            total = term if total is None else total + term
        gr[i] = total
        grrecv[i, t] = total
        loop(1, n, lambda s: gr_copy(i, peer_t(s), t).start())

        def block_a(j):
            if i == 0:
                x_copy(j).wait()
            two = stacked(lg[i, j]).T.astype(jnp.bfloat16)
            lcat = jnp.concatenate([two, two], axis=1)
            at = rows_of(j)
            sums = jnp.zeros((lc, 2 * rank), jnp.float32)
            for b in range(times // width):
                part = pl.ds(b * width, width)
                values = x[at, part]
                residue = values - dot(lcat, rcat[:, part])
                outlier = residue - jnp.clip(residue, -LEVEL, LEVEL)
                high, low = split(values - outlier)
                if last:
                    x[at, part] = outlier
                clean[0, at, part] = high
                clean[1, at, part] = low
                sums += dot(high, rwide[part, :]) + dot(low, rwide[part, :])
            flat = sums.T
            sbuf[i, j] = flat[:rank] + flat[rank:]

        def own_a(s):
            block_a(mine(first_of(0, s) if i == 0 else flip(s)))

        def other_a(s):
            q = flip(s)
            if i == 0:
                left_wait_other(0, q)
            block_a(theirs(q))
            pair_copy(i, q, q).start()

        def join(s):
            q = flip(s)
            pair_copy(i, q, q).wait_recv()
            sbuf[i, mine(q)] += precv[i, q]

            @pl.when(s > 0)
            def _():
                s_copy(i, q, z).start()

        def own_join(s):
            own_a(half - 1 - s)
            join(half - 1 - s)

        if i == 0:
            loop(0, half, own_a)
            loop(0, half, lambda s: other_a(half - 1 - s))
            loop(0, half, lambda s: join(half - 1 - s))
        else:
            loop(0, half, lambda s: other_a(half - 1 - s))
            loop(0, half, own_join)

        loop(1, n, lambda s: gr_copy(i, t, peer_t(s)).wait_recv())
        total = ridge
        for q in range(n):
            total = total + grrecv[i, q]
        inv_r[...] = inverse(total)

        def add_s(s, value):
            q = flip(s)
            s_copy(i, z, q).wait_recv()
            return value + srecv[i, q]

        total = lax.fori_loop(1, half, add_s, sbuf[i, t])
        piece = jnp.dot(inv_r[...], total, precision=HIGHEST, preferred_element_type=jnp.float32)
        lg[i + 1, t] = piece
        left_send(i + 1)
        if last:
            lout[...] = piece

        acc[...] = jnp.zeros_like(acc)

        def block_b(j, gram):
            value = lg[i + 1, j]
            both = stacked(value).astype(jnp.bfloat16)
            at = rows_of(j)
            for b in range(times // width):
                part = pl.ds(b * width, width)
                acc[:, part] += dot(both, clean[0, at, part]) + dot(both, clean[1, at, part])
            return gram + outer_gram(value)

        def own_b(s, gram):
            return block_b(mine(first_of(i + 1, s)), gram)

        def other_b(s, gram):
            q = flip(s)
            left_wait_other(i + 1, q)
            return block_b(theirs(q), gram)

        gram = lax.fori_loop(0, half, own_b, jnp.zeros((rank, rank), jnp.float32))
        gram = lax.fori_loop(0, half, other_b, gram)
        gl[i] = gram
        glrecv[i, c] = gram
        loop(1, m, lambda s: gl_copy(i, peer_c(s), c).start())
        for q in range(m):
            at = pl.ds(q * rc, rc)
            tbuf[i, q] = acc[:rank, at] + acc[rank:, at]
        loop(1, m, lambda s: t_copy(i, peer_c(s), c).start())
        loop(1, m, lambda s: gl_copy(i, c, peer_c(s)).wait_recv())
        total = ridge
        for q in range(m):
            total = total + glrecv[i, q]
        inv_l = inverse(total)

        def add_t(s, value):
            j = peer_c(s)
            t_copy(i, c, j).wait_recv()
            return value + trecv[i, j]

        total = lax.fori_loop(1, m, add_t, tbuf[i, c])
        piece = jnp.dot(inv_l, total, precision=HIGHEST, preferred_element_type=jnp.float32)
        if last:
            rout[...] = piece
        else:
            rg[i + 1, c] = piece
            loop(1, m, lambda s: right_copy(i + 1, peer_c(s), c).start())

    for i in range(ITERS):
        loop(0, half, lambda s: pair_copy(i, s, s).wait_send())
        loop(1, half, lambda s: s_copy(i, flip(s), z).wait_send())
        loop(1, n, lambda s: gr_copy(i, peer_t(s), t).wait_send())
        loop(1, m, lambda s: t_copy(i, peer_c(s), c).wait_send())
        loop(1, m, lambda s: gl_copy(i, peer_c(s), c).wait_send())
        loop(1, m, lambda s: right_copy(i, peer_c(s), c).wait_send())
    for g in range(ITERS + 1):
        loop(1, half, lambda s: left_z(g, flip(s), t).wait_send())
        loop(0, half, lambda s: left_x(g, s, t, False).wait_send())


def shards(n, m, readings, channel_start, time_start):
    lc, rank = channel_start.shape
    rc = time_start.shape[0]
    rows, times = readings.shape
    f32 = jnp.float32
    vmem = pl.BlockSpec(memory_space=pltpu.VMEM)
    anywhere = pl.BlockSpec(memory_space=pltpu.HBM)
    dma = pltpu.SemaphoreType.DMA
    outliers, left, right = pl.pallas_call(
        functools.partial(kernel, n, m),
        out_shape=(jax.ShapeDtypeStruct((rows, times), f32),
                   jax.ShapeDtypeStruct((rank, lc), f32),
                   jax.ShapeDtypeStruct((rank, rc), f32)),
        in_specs=[anywhere, vmem, vmem],
        out_specs=(vmem, vmem, vmem),
        scratch_shapes=[
            pltpu.VMEM((2, rows, times), jnp.bfloat16),
            pltpu.VMEM((ITERS + 1, n, rank, lc), f32),
            pltpu.VMEM((ITERS, n, rank, lc), f32),
            pltpu.VMEM((ITERS, n // 2, rank, lc), f32),
            pltpu.VMEM((ITERS, n // 2, rank, lc), f32),
            pltpu.VMEM((ITERS, m, rank, rc), f32),
            pltpu.VMEM((ITERS, m, rank, rc), f32),
            pltpu.VMEM((ITERS, m, rank, rc), f32),
            pltpu.VMEM((ITERS, rank, rank), f32),
            pltpu.VMEM((ITERS, rank, rank), f32),
            pltpu.VMEM((ITERS, m, rank, rank), f32),
            pltpu.VMEM((ITERS, n, rank, rank), f32),
            pltpu.VMEM((4 * rank, times), jnp.bfloat16),
            pltpu.VMEM((times, 2 * rank), jnp.bfloat16),
            pltpu.VMEM((2 * rank, times), f32),
            pltpu.VMEM((rank, rank), f32),
            dma((ITERS + 1, n // 2)), dma((ITERS + 1, n // 2)), dma((ITERS + 1, n)),
            dma((ITERS, n // 2)), dma((ITERS, n // 2)),
            dma((ITERS, n // 2)), dma((ITERS, n // 2)),
            dma((ITERS, m)), dma((ITERS, m)),
            dma((ITERS, m)), dma((ITERS, m)),
            dma((ITERS, m)), dma((ITERS, m)),
            dma((ITERS, n)), dma((ITERS, n)),
            dma((n,)),
        ],
        compiler_params=pltpu.CompilerParams(collective_id=0, has_side_effects=True,
                                             vmem_limit_bytes=32 * 1024 * 1024),
    )(readings, channel_start.T, time_start.T)
    return outliers, left.T, right.T


def solution(mesh):
    n, m = mesh.shape["tm"], mesh.shape["chan"]
    specs = (P("chan", "tm"), P(("chan", "tm"), None), P(("tm", "chan"), None))
    return jax.shard_map(functools.partial(shards, n, m), mesh=mesh, in_specs=specs, out_specs=specs,
                         check_vma=False)
```

```python
import functools

import jax
import jax.numpy as jnp
from jax import lax
from jax.experimental import pallas as pl
from jax.experimental.pallas import tpu as pltpu
from jax.sharding import PartitionSpec as P

ITERS = 2
LEVEL = 1.5
RIDGE = 8.0
MESH = pl.DeviceIdType.MESH
HIGHEST = lax.Precision.HIGHEST


def split(value):
    high = value.astype(jnp.bfloat16)
    low = (value - high.astype(jnp.float32)).astype(jnp.bfloat16)
    return high, low


def stacked(value):
    high = value.astype(jnp.bfloat16).astype(jnp.float32)
    return jnp.concatenate([high, value - high], axis=0)


def dot(first, second):
    return jnp.dot(first, second, preferred_element_type=jnp.float32)


def outer_gram(value):
    return lax.dot_general(value, value, (((1,), (1,)), ((), ())), precision=HIGHEST,
                           preferred_element_type=jnp.float32)


def packed(gram):
    half = gram.shape[0] // 2
    return jnp.concatenate([gram[:half], gram[half:]], axis=1)


def unpacked(value):
    rank = value.shape[0] * 2
    return jnp.concatenate([value[:, :rank], value[:, rank:]], axis=0)


def inverse(gram):
    rank = gram.shape[0]
    rows = lax.broadcasted_iota(jnp.int32, (rank, rank), 0)
    cols = lax.broadcasted_iota(jnp.int32, (rank, rank), 1)
    lane = cols[:1]
    for k in range(0, rank, 2):
        up, down = gram[k:k + 1, :], gram[k + 1:k + 2, :]
        first, second = gram[:, k:k + 1], gram[:, k + 1:k + 2]
        wide = lambda value: jnp.broadcast_to(value, (1, rank))
        p, q = wide(up[:, k:k + 1]), wide(up[:, k + 1:k + 2])
        r, d = wide(down[:, k:k + 1]), wide(down[:, k + 1:k + 2])
        inv = 1.0 / (p * d - q * r)
        up = jnp.where(lane == k, 1.0, jnp.where(lane == k + 1, 0.0, up))
        down = jnp.where(lane == k, 0.0, jnp.where(lane == k + 1, 1.0, down))
        new_up = (d * up - q * down) * inv
        new_down = (p * down - r * up) * inv
        rest = jnp.where((cols == k) | (cols == k + 1), 0.0, gram) - first * new_up - second * new_down
        gram = jnp.where(rows == k, new_up, jnp.where(rows == k + 1, new_down, rest))
    return gram


def kernel(n, m, x_hbm, l0, r0, x, lout, rout,
           clean, lg, sbuf, precv, srecv, rg, tbuf, trecv, gl, gr, glrecv, grrecv,
           rcat, rwide, acc, inv_r,
           lz_s, lx_s, l_r, p_s, p_r, s_s, s_r, t_s, t_r, r_s, r_r, gl_s, gl_r, gr_s, gr_r, x_sem):
    c = lax.axis_index("chan")
    t = lax.axis_index("tm")
    rank, lc = l0.shape
    rc = r0.shape[1]
    times = x.shape[1]
    width = times
    half = n // 2
    z, pair = t // 2, t % 2
    other = z * 2 + 1 - pair

    def flip(s):
        value, bit = 0, 1
        while bit < half:
            value = value + bit * ((z // bit + s // bit) % 2)
            bit *= 2
        return value

    def mine(q):
        return q * 2 + pair

    def theirs(q):
        return q * 2 + 1 - pair

    def peer_t(s):
        return lax.rem(t + s, n)

    def peer_c(s):
        return lax.rem(c + s, m)

    def copy_t(src, dst, ssem, rsem, j):
        return pltpu.make_async_remote_copy(src_ref=src, dst_ref=dst, send_sem=ssem, recv_sem=rsem,
                                            device_id=(c, j), device_id_type=MESH)

    def copy_c(src, dst, ssem, rsem, j):
        return pltpu.make_async_remote_copy(src_ref=src, dst_ref=dst, send_sem=ssem, recv_sem=rsem,
                                            device_id=(j, t), device_id_type=MESH)

    def loop(first, last, body):
        def step(s, carry):
            body(s)
            return carry
        lax.fori_loop(first, last, step, 0)

    def left_src(g, q, own):
        return l0 if own and g == 0 else lg.at[g, mine(q)]

    def left_z(g, q, slot, own=True):
        return copy_t(left_src(g, z, own), lg.at[g, slot], lz_s.at[g, q], l_r.at[g, slot], mine(q))

    def left_x(g, q, slot, own):
        return copy_t(left_src(g, q, own), lg.at[g, slot], lx_s.at[g, q], l_r.at[g, slot], other)

    def left_send(g):
        loop(1, half, lambda s: left_z(g, flip(s), t).start())
        left_x(g, z, t, True).start()

    def left_wait(g, q):
        left_z(g, q, mine(q)).wait_recv()
        left_x(g, q, mine(q), False).start()

    def left_wait_other(g, q):
        left_x(g, q, theirs(q), False).wait_recv()

    def pair_copy(i, q, slot):
        return copy_t(sbuf.at[i, theirs(q)], precv.at[i, slot], p_s.at[i, q], p_r.at[i, slot], other)

    def s_copy(i, q, slot):
        return copy_t(sbuf.at[i, mine(q)], srecv.at[i, slot], s_s.at[i, q], s_r.at[i, slot], mine(q))

    def gr_copy(i, j, slot):
        return copy_t(gr.at[i], grrecv.at[i, slot], gr_s.at[i, j], gr_r.at[i, slot], j)

    def right_copy(g, j, slot):
        src = r0 if g == 0 else rg.at[g, c]
        return copy_c(src, rg.at[g, slot], r_s.at[g, j], r_r.at[g, slot], j)

    def t_copy(i, j, slot):
        return copy_c(tbuf.at[i, j], trecv.at[i, slot], t_s.at[i, j], t_r.at[i, slot], j)

    def gl_copy(i, j, slot):
        return copy_c(gl.at[i], glrecv.at[i, slot], gl_s.at[i, j], gl_r.at[i, slot], j)

    def rows_of(j):
        return pl.ds(pl.multiple_of(j * lc, lc), lc)

    def x_copy(j):
        return pltpu.make_async_copy(x_hbm.at[rows_of(j)], x.at[rows_of(j)], x_sem.at[j])

    def first_of(i, s):
        q = flip(s)

        @pl.when(s > 0)
        def _():
            left_wait(i, q)
        return q

    loop(0, half, lambda s: x_copy(mine(flip(s))).start())
    loop(0, half, lambda s: x_copy(theirs(flip(s))).start())

    barrier = pltpu.get_barrier_semaphore()
    loop(1, n, lambda s: pl.semaphore_signal(barrier, inc=1, device_id=(c, peer_t(s)), device_id_type=MESH))
    loop(1, m, lambda s: pl.semaphore_signal(barrier, inc=1, device_id=(peer_c(s), t), device_id_type=MESH))
    pl.semaphore_wait(barrier, n + m - 2)

    loop(1, m, lambda s: right_copy(0, peer_c(s), c).start())
    left_send(0)
    lg[0, t] = l0[...]
    rg[0, c] = r0[...]

    rows = lax.broadcasted_iota(jnp.int32, (rank, rank), 0)
    cols = lax.broadcasted_iota(jnp.int32, (rank, rank), 1)
    ridge = jnp.where(rows == cols, RIDGE, 0.0).astype(jnp.float32)

    for i in range(ITERS):
        last = i == ITERS - 1

        loop(1, m, lambda s: right_copy(i, c, peer_c(s)).wait_recv())
        total = None
        for q in range(m):
            part = rg[i, q]
            both = stacked(part)
            high = both[:rank]
            low = both[rank:]
            at = pl.ds(q * rc, rc)
            rcat[:, at] = jnp.concatenate([high, high, low, low], axis=0).astype(jnp.bfloat16)
            rwide[at, :] = both.T.astype(jnp.bfloat16)
            term = outer_gram(part)
            total = term if total is None else total + term
        total = packed(total)
        gr[i] = total
        grrecv[i, t] = total
        loop(1, n, lambda s: gr_copy(i, peer_t(s), t).start())

        def block_a(j):
            if i == 0:
                x_copy(j).wait()
            two = stacked(lg[i, j]).T.astype(jnp.bfloat16)
            lcat = jnp.concatenate([two, two], axis=1)
            at = rows_of(j)
            sums = jnp.zeros((lc, 2 * rank), jnp.float32)
            for b in range(times // width):
                part = pl.ds(b * width, width)
                values = x[at, part]
                residue = values - dot(lcat, rcat[:, part])
                outlier = residue - jnp.clip(residue, -LEVEL, LEVEL)
                high, low = split(values - outlier)
                if last:
                    x[at, part] = outlier
                clean[0, at, part] = high
                clean[1, at, part] = low
                sums += dot(high, rwide[part, :]) + dot(low, rwide[part, :])
            flat = sums.T
            sbuf[i, j] = flat[:rank] + flat[rank:]

        def own_a(s):
            block_a(mine(first_of(0, s) if i == 0 else flip(s)))

        def other_a(s):
            q = flip(s)
            if i == 0:
                left_wait_other(0, q)
            block_a(theirs(q))
            pair_copy(i, q, q).start()

        def join(s):
            q = flip(s)
            pair_copy(i, q, q).wait_recv()
            sbuf[i, mine(q)] += precv[i, q]

            @pl.when(s > 0)
            def _():
                s_copy(i, q, z).start()

        def own_join(s):
            own_a(half - 1 - s)
            join(half - 1 - s)

        if i == 0:
            loop(0, half, own_a)
            loop(0, half, lambda s: other_a(half - 1 - s))
            loop(0, half, lambda s: join(half - 1 - s))
        else:
            loop(0, half, lambda s: other_a(half - 1 - s))
            loop(0, half, own_join)

        loop(1, n, lambda s: gr_copy(i, t, peer_t(s)).wait_recv())
        total = grrecv[i, 0]
        for q in range(1, n):
            total = total + grrecv[i, q]
        inv_r[...] = inverse(unpacked(total) + ridge)

        def add_s(s, value):
            q = flip(s)
            s_copy(i, z, q).wait_recv()
            return value + srecv[i, q]

        total = lax.fori_loop(1, half, add_s, sbuf[i, t])
        piece = jnp.dot(inv_r[...], total, precision=HIGHEST, preferred_element_type=jnp.float32)
        lg[i + 1, t] = piece
        left_send(i + 1)
        if last:
            lout[...] = piece

        acc[...] = jnp.zeros_like(acc)

        def block_b(j, gram):
            value = lg[i + 1, j]
            both = stacked(value).astype(jnp.bfloat16)
            at = rows_of(j)
            for b in range(times // width):
                part = pl.ds(b * width, width)
                acc[:, part] += dot(both, clean[0, at, part]) + dot(both, clean[1, at, part])
            return gram + outer_gram(value)

        def own_b(s, gram):
            return block_b(mine(first_of(i + 1, s)), gram)

        def other_b(s, gram):
            q = flip(s)
            left_wait_other(i + 1, q)
            return block_b(theirs(q), gram)

        gram = lax.fori_loop(0, half, own_b, jnp.zeros((rank, rank), jnp.float32))
        gram = lax.fori_loop(0, half, other_b, gram)
        gram = packed(gram)
        gl[i] = gram
        glrecv[i, c] = gram
        loop(1, m, lambda s: gl_copy(i, peer_c(s), c).start())
        for q in range(m):
            at = pl.ds(q * rc, rc)
            tbuf[i, q] = acc[:rank, at] + acc[rank:, at]
        loop(1, m, lambda s: t_copy(i, peer_c(s), c).start())
        loop(1, m, lambda s: gl_copy(i, c, peer_c(s)).wait_recv())
        total = glrecv[i, 0]
        for q in range(1, m):
            total = total + glrecv[i, q]
        inv_l = inverse(unpacked(total) + ridge)

        def add_t(s, value):
            j = peer_c(s)
            t_copy(i, c, j).wait_recv()
            return value + trecv[i, j]

        total = lax.fori_loop(1, m, add_t, tbuf[i, c])
        piece = jnp.dot(inv_l, total, precision=HIGHEST, preferred_element_type=jnp.float32)
        if last:
            rout[...] = piece
        else:
            rg[i + 1, c] = piece
            loop(1, m, lambda s: right_copy(i + 1, peer_c(s), c).start())

    for i in range(ITERS):
        loop(0, half, lambda s: pair_copy(i, s, s).wait_send())
        loop(1, half, lambda s: s_copy(i, flip(s), z).wait_send())
        loop(1, n, lambda s: gr_copy(i, peer_t(s), t).wait_send())
        loop(1, m, lambda s: t_copy(i, peer_c(s), c).wait_send())
        loop(1, m, lambda s: gl_copy(i, peer_c(s), c).wait_send())
        loop(1, m, lambda s: right_copy(i, peer_c(s), c).wait_send())
    for g in range(ITERS + 1):
        loop(1, half, lambda s: left_z(g, flip(s), t).wait_send())
        loop(0, half, lambda s: left_x(g, s, t, False).wait_send())


def shards(n, m, readings, channel_start, time_start):
    lc, rank = channel_start.shape
    rc = time_start.shape[0]
    rows, times = readings.shape
    f32 = jnp.float32
    vmem = pl.BlockSpec(memory_space=pltpu.VMEM)
    anywhere = pl.BlockSpec(memory_space=pltpu.HBM)
    dma = pltpu.SemaphoreType.DMA
    outliers, left, right = pl.pallas_call(
        functools.partial(kernel, n, m),
        out_shape=(jax.ShapeDtypeStruct((rows, times), f32),
                   jax.ShapeDtypeStruct((rank, lc), f32),
                   jax.ShapeDtypeStruct((rank, rc), f32)),
        in_specs=[anywhere, vmem, vmem],
        out_specs=(vmem, vmem, vmem),
        scratch_shapes=[
            pltpu.VMEM((2, rows, times), jnp.bfloat16),
            pltpu.VMEM((ITERS + 1, n, rank, lc), f32),
            pltpu.VMEM((ITERS, n, rank, lc), f32),
            pltpu.VMEM((ITERS, n // 2, rank, lc), f32),
            pltpu.VMEM((ITERS, n // 2, rank, lc), f32),
            pltpu.VMEM((ITERS, m, rank, rc), f32),
            pltpu.VMEM((ITERS, m, rank, rc), f32),
            pltpu.VMEM((ITERS, m, rank, rc), f32),
            pltpu.VMEM((ITERS, rank // 2, 2 * rank), f32),
            pltpu.VMEM((ITERS, rank // 2, 2 * rank), f32),
            pltpu.VMEM((ITERS, m, rank // 2, 2 * rank), f32),
            pltpu.VMEM((ITERS, n, rank // 2, 2 * rank), f32),
            pltpu.VMEM((4 * rank, times), jnp.bfloat16),
            pltpu.VMEM((times, 2 * rank), jnp.bfloat16),
            pltpu.VMEM((2 * rank, times), f32),
            pltpu.VMEM((rank, rank), f32),
            dma((ITERS + 1, n // 2)), dma((ITERS + 1, n // 2)), dma((ITERS + 1, n)),
            dma((ITERS, n // 2)), dma((ITERS, n // 2)),
            dma((ITERS, n // 2)), dma((ITERS, n // 2)),
            dma((ITERS, m)), dma((ITERS, m)),
            dma((ITERS, m)), dma((ITERS, m)),
            dma((ITERS, m)), dma((ITERS, m)),
            dma((ITERS, n)), dma((ITERS, n)),
            dma((n,)),
        ],
        compiler_params=pltpu.CompilerParams(collective_id=0, has_side_effects=True,
                                             vmem_limit_bytes=42 * 1024 * 1024),
    )(readings, channel_start.T, time_start.T)
    return outliers, left.T, right.T


def solution(mesh):
    n, m = mesh.shape["tm"], mesh.shape["chan"]
    specs = (P("chan", "tm"), P(("chan", "tm"), None), P(("tm", "chan"), None))
    return jax.shard_map(functools.partial(shards, n, m), mesh=mesh, in_specs=specs, out_specs=specs,
                         check_vma=False)
```

```python
import functools

import jax
import jax.numpy as jnp
from jax import lax
from jax.experimental import pallas as pl
from jax.experimental.pallas import tpu as pltpu
from jax.sharding import PartitionSpec as P

ITERS = 2
LEVEL = 1.5
RIDGE = 8.0
MESH = pl.DeviceIdType.MESH
HIGHEST = lax.Precision.HIGHEST


def split(value):
    high = value.astype(jnp.bfloat16)
    low = (value - high.astype(jnp.float32)).astype(jnp.bfloat16)
    return high, low


def stacked(value):
    high = value.astype(jnp.bfloat16).astype(jnp.float32)
    return jnp.concatenate([high, value - high], axis=0)


def dot(first, second):
    return jnp.dot(first, second, preferred_element_type=jnp.float32)


def outer_gram(both):
    return lax.dot_general(both, both, (((1,), (1,)), ((), ())), preferred_element_type=jnp.float32)


def packed(parts):
    rank = parts.shape[0] // 2
    half = rank // 2
    gram = (parts[:rank, :rank] + parts[rank:, rank:]) + (parts[:rank, rank:] + parts[rank:, :rank])
    return jnp.concatenate([gram[:half], gram[half:]], axis=1)


def unpacked(value):
    rank = value.shape[0] * 2
    return jnp.concatenate([value[:, :rank], value[:, rank:]], axis=0)


def inverse(gram):
    rank = gram.shape[0]
    rows = lax.broadcasted_iota(jnp.int32, (rank, rank), 0)
    cols = lax.broadcasted_iota(jnp.int32, (rank, rank), 1)
    lane = cols[:1]
    for k in range(0, rank, 2):
        up, down = gram[k:k + 1, :], gram[k + 1:k + 2, :]
        first, second = gram[:, k:k + 1], gram[:, k + 1:k + 2]
        wide = lambda value: jnp.broadcast_to(value, (1, rank))
        p, q = wide(up[:, k:k + 1]), wide(up[:, k + 1:k + 2])
        r, d = wide(down[:, k:k + 1]), wide(down[:, k + 1:k + 2])
        inv = 1.0 / (p * d - q * r)
        up = jnp.where(lane == k, 1.0, jnp.where(lane == k + 1, 0.0, up))
        down = jnp.where(lane == k, 0.0, jnp.where(lane == k + 1, 1.0, down))
        new_up = (d * up - q * down) * inv
        new_down = (p * down - r * up) * inv
        rest = jnp.where((cols == k) | (cols == k + 1), 0.0, gram) - first * new_up - second * new_down
        gram = jnp.where(rows == k, new_up, jnp.where(rows == k + 1, new_down, rest))
    return gram


def kernel(n, m, x_hbm, l0, r0, x, lout, rout,
           clean, lg, sbuf, precv, srecv, rg, tbuf, trecv, gl, gr, glrecv, grrecv,
           rcat, rwide, acc, inv_r,
           lz_s, lx_s, l_r, p_s, p_r, s_s, s_r, t_s, t_r, r_s, r_r, gl_s, gl_r, gr_s, gr_r, x_sem):
    c = lax.axis_index("chan")
    t = lax.axis_index("tm")
    rank, lc = l0.shape
    rc = r0.shape[1]
    times = x.shape[1]
    width = times
    half = n // 2
    z, pair = t // 2, t % 2
    other = z * 2 + 1 - pair

    def flip(s):
        value, bit = 0, 1
        while bit < half:
            value = value + bit * ((z // bit + s // bit) % 2)
            bit *= 2
        return value

    def mine(q):
        return q * 2 + pair

    def theirs(q):
        return q * 2 + 1 - pair

    def peer_t(s):
        return lax.rem(t + s, n)

    def peer_c(s):
        return lax.rem(c + s, m)

    def copy_t(src, dst, ssem, rsem, j):
        return pltpu.make_async_remote_copy(src_ref=src, dst_ref=dst, send_sem=ssem, recv_sem=rsem,
                                            device_id=(c, j), device_id_type=MESH)

    def copy_c(src, dst, ssem, rsem, j):
        return pltpu.make_async_remote_copy(src_ref=src, dst_ref=dst, send_sem=ssem, recv_sem=rsem,
                                            device_id=(j, t), device_id_type=MESH)

    def loop(first, last, body):
        def step(s, carry):
            body(s)
            return carry
        lax.fori_loop(first, last, step, 0)

    def left_src(g, q, own):
        return l0 if own and g == 0 else lg.at[g, mine(q)]

    def left_z(g, q, slot, own=True):
        return copy_t(left_src(g, z, own), lg.at[g, slot], lz_s.at[g, q], l_r.at[g, slot], mine(q))

    def left_x(g, q, slot, own):
        return copy_t(left_src(g, q, own), lg.at[g, slot], lx_s.at[g, q], l_r.at[g, slot], other)

    def left_send(g):
        loop(1, half, lambda s: left_z(g, flip(s), t).start())
        left_x(g, z, t, True).start()

    def left_wait(g, q):
        left_z(g, q, mine(q)).wait_recv()
        left_x(g, q, mine(q), False).start()

    def left_wait_other(g, q):
        left_x(g, q, theirs(q), False).wait_recv()

    def pair_copy(i, q, slot):
        return copy_t(sbuf.at[i, theirs(q)], precv.at[i, slot], p_s.at[i, q], p_r.at[i, slot], other)

    def s_copy(i, q, slot):
        return copy_t(sbuf.at[i, mine(q)], srecv.at[i, slot], s_s.at[i, q], s_r.at[i, slot], mine(q))

    def gr_copy(i, j, slot):
        return copy_t(gr.at[i], grrecv.at[i, slot], gr_s.at[i, j], gr_r.at[i, slot], j)

    def right_copy(g, j, slot):
        src = r0 if g == 0 else rg.at[g, c]
        return copy_c(src, rg.at[g, slot], r_s.at[g, j], r_r.at[g, slot], j)

    def t_copy(i, j, slot):
        return copy_c(tbuf.at[i, j], trecv.at[i, slot], t_s.at[i, j], t_r.at[i, slot], j)

    def gl_copy(i, j, slot):
        return copy_c(gl.at[i], glrecv.at[i, slot], gl_s.at[i, j], gl_r.at[i, slot], j)

    def rows_of(j):
        return pl.ds(pl.multiple_of(j * lc, lc), lc)

    def x_copy(j):
        return pltpu.make_async_copy(x_hbm.at[rows_of(j)], x.at[rows_of(j)], x_sem.at[j])

    def first_of(i, s):
        q = flip(s)

        @pl.when(s > 0)
        def _():
            left_wait(i, q)
        return q

    loop(0, half, lambda s: x_copy(mine(flip(s))).start())
    loop(0, half, lambda s: x_copy(theirs(flip(s))).start())

    barrier = pltpu.get_barrier_semaphore()
    loop(1, n, lambda s: pl.semaphore_signal(barrier, inc=1, device_id=(c, peer_t(s)), device_id_type=MESH))
    loop(1, m, lambda s: pl.semaphore_signal(barrier, inc=1, device_id=(peer_c(s), t), device_id_type=MESH))
    pl.semaphore_wait(barrier, n + m - 2)

    loop(1, m, lambda s: right_copy(0, peer_c(s), c).start())
    left_send(0)
    lg[0, t] = l0[...]
    rg[0, c] = r0[...]

    rows = lax.broadcasted_iota(jnp.int32, (rank, rank), 0)
    cols = lax.broadcasted_iota(jnp.int32, (rank, rank), 1)
    ridge = jnp.where(rows == cols, RIDGE, 0.0).astype(jnp.float32)

    for i in range(ITERS):
        last = i == ITERS - 1

        loop(1, m, lambda s: right_copy(i, c, peer_c(s)).wait_recv())
        total = None
        for q in range(m):
            part = rg[i, q]
            both = stacked(part)
            high = both[:rank]
            low = both[rank:]
            at = pl.ds(q * rc, rc)
            rcat[:, at] = jnp.concatenate([high, high, low, low], axis=0).astype(jnp.bfloat16)
            rwide[at, :] = both.T.astype(jnp.bfloat16)
            term = outer_gram(both.astype(jnp.bfloat16))
            total = term if total is None else total + term
        total = packed(total)
        gr[i] = total
        grrecv[i, t] = total
        loop(1, n, lambda s: gr_copy(i, peer_t(s), t).start())

        def block_a(j):
            if i == 0:
                x_copy(j).wait()
            two = stacked(lg[i, j]).T.astype(jnp.bfloat16)
            lcat = jnp.concatenate([two, two], axis=1)
            at = rows_of(j)
            sums = jnp.zeros((lc, 2 * rank), jnp.float32)
            for b in range(times // width):
                part = pl.ds(b * width, width)
                values = x[at, part]
                fitted = dot(lcat, rcat[:, part])
                residue = values - fitted
                clipped = jnp.clip(residue, -LEVEL, LEVEL)
                high, low = split(fitted + clipped)
                if last:
                    x[at, part] = residue - clipped
                clean[0, at, part] = high
                clean[1, at, part] = low
                sums += dot(high, rwide[part, :]) + dot(low, rwide[part, :])
            flat = sums.T
            sbuf[i, j] = flat[:rank] + flat[rank:]

        def own_a(s):
            block_a(mine(first_of(0, s) if i == 0 else flip(s)))

        def other_a(s):
            q = flip(s)
            if i == 0:
                left_wait_other(0, q)
            block_a(theirs(q))
            pair_copy(i, q, q).start()

        def join(s):
            q = flip(s)
            pair_copy(i, q, q).wait_recv()
            sbuf[i, mine(q)] += precv[i, q]

            @pl.when(s > 0)
            def _():
                s_copy(i, q, z).start()

        def own_join(s):
            own_a(half - 1 - s)
            join(half - 1 - s)

        if i == 0:
            loop(0, half, own_a)
            loop(0, half, lambda s: other_a(half - 1 - s))
            loop(0, half, lambda s: join(half - 1 - s))
        else:
            loop(0, half, lambda s: other_a(half - 1 - s))
            loop(0, half, own_join)

        loop(1, n, lambda s: gr_copy(i, t, peer_t(s)).wait_recv())
        total = grrecv[i, 0]
        for q in range(1, n):
            total = total + grrecv[i, q]
        inv_r[...] = inverse(unpacked(total) + ridge)

        def add_s(s, value):
            q = flip(s)
            s_copy(i, z, q).wait_recv()
            return value + srecv[i, q]

        total = lax.fori_loop(1, half, add_s, sbuf[i, t])
        piece = jnp.dot(inv_r[...], total, precision=HIGHEST, preferred_element_type=jnp.float32)
        lg[i + 1, t] = piece
        left_send(i + 1)
        if last:
            lout[...] = piece

        acc[...] = jnp.zeros_like(acc)

        def block_b(j, gram):
            value = lg[i + 1, j]
            both = stacked(value).astype(jnp.bfloat16)
            at = rows_of(j)
            for b in range(times // width):
                part = pl.ds(b * width, width)
                acc[:, part] += dot(both, clean[0, at, part]) + dot(both, clean[1, at, part])
            return gram + outer_gram(both)

        def own_b(s, gram):
            return block_b(mine(first_of(i + 1, s)), gram)

        def other_b(s, gram):
            q = flip(s)
            left_wait_other(i + 1, q)
            return block_b(theirs(q), gram)

        gram = lax.fori_loop(0, half, own_b, jnp.zeros((2 * rank, 2 * rank), jnp.float32))
        gram = lax.fori_loop(0, half, other_b, gram)
        gram = packed(gram)
        gl[i] = gram
        glrecv[i, c] = gram
        loop(1, m, lambda s: gl_copy(i, peer_c(s), c).start())
        for q in range(m):
            at = pl.ds(q * rc, rc)
            tbuf[i, q] = acc[:rank, at] + acc[rank:, at]
        loop(1, m, lambda s: t_copy(i, peer_c(s), c).start())
        loop(1, m, lambda s: gl_copy(i, c, peer_c(s)).wait_recv())
        total = glrecv[i, 0]
        for q in range(1, m):
            total = total + glrecv[i, q]
        inv_l = inverse(unpacked(total) + ridge)

        def add_t(s, value):
            j = peer_c(s)
            t_copy(i, c, j).wait_recv()
            return value + trecv[i, j]

        total = lax.fori_loop(1, m, add_t, tbuf[i, c])
        piece = jnp.dot(inv_l, total, precision=HIGHEST, preferred_element_type=jnp.float32)
        if last:
            rout[...] = piece
        else:
            rg[i + 1, c] = piece
            loop(1, m, lambda s: right_copy(i + 1, peer_c(s), c).start())

    for i in range(ITERS):
        loop(0, half, lambda s: pair_copy(i, s, s).wait_send())
        loop(1, half, lambda s: s_copy(i, flip(s), z).wait_send())
        loop(1, n, lambda s: gr_copy(i, peer_t(s), t).wait_send())
        loop(1, m, lambda s: t_copy(i, peer_c(s), c).wait_send())
        loop(1, m, lambda s: gl_copy(i, peer_c(s), c).wait_send())
        loop(1, m, lambda s: right_copy(i, peer_c(s), c).wait_send())
    for g in range(ITERS + 1):
        loop(1, half, lambda s: left_z(g, flip(s), t).wait_send())
        loop(0, half, lambda s: left_x(g, s, t, False).wait_send())


def shards(n, m, readings, channel_start, time_start):
    lc, rank = channel_start.shape
    rc = time_start.shape[0]
    rows, times = readings.shape
    f32 = jnp.float32
    vmem = pl.BlockSpec(memory_space=pltpu.VMEM)
    anywhere = pl.BlockSpec(memory_space=pltpu.HBM)
    dma = pltpu.SemaphoreType.DMA
    outliers, left, right = pl.pallas_call(
        functools.partial(kernel, n, m),
        out_shape=(jax.ShapeDtypeStruct((rows, times), f32),
                   jax.ShapeDtypeStruct((rank, lc), f32),
                   jax.ShapeDtypeStruct((rank, rc), f32)),
        in_specs=[anywhere, vmem, vmem],
        out_specs=(vmem, vmem, vmem),
        scratch_shapes=[
            pltpu.VMEM((2, rows, times), jnp.bfloat16),
            pltpu.VMEM((ITERS + 1, n, rank, lc), f32),
            pltpu.VMEM((ITERS, n, rank, lc), f32),
            pltpu.VMEM((ITERS, n // 2, rank, lc), f32),
            pltpu.VMEM((ITERS, n // 2, rank, lc), f32),
            pltpu.VMEM((ITERS, m, rank, rc), f32),
            pltpu.VMEM((ITERS, m, rank, rc), f32),
            pltpu.VMEM((ITERS, m, rank, rc), f32),
            pltpu.VMEM((ITERS, rank // 2, 2 * rank), f32),
            pltpu.VMEM((ITERS, rank // 2, 2 * rank), f32),
            pltpu.VMEM((ITERS, m, rank // 2, 2 * rank), f32),
            pltpu.VMEM((ITERS, n, rank // 2, 2 * rank), f32),
            pltpu.VMEM((4 * rank, times), jnp.bfloat16),
            pltpu.VMEM((times, 2 * rank), jnp.bfloat16),
            pltpu.VMEM((2 * rank, times), f32),
            pltpu.VMEM((rank, rank), f32),
            dma((ITERS + 1, n // 2)), dma((ITERS + 1, n // 2)), dma((ITERS + 1, n)),
            dma((ITERS, n // 2)), dma((ITERS, n // 2)),
            dma((ITERS, n // 2)), dma((ITERS, n // 2)),
            dma((ITERS, m)), dma((ITERS, m)),
            dma((ITERS, m)), dma((ITERS, m)),
            dma((ITERS, m)), dma((ITERS, m)),
            dma((ITERS, n)), dma((ITERS, n)),
            dma((n,)),
        ],
        compiler_params=pltpu.CompilerParams(collective_id=0, has_side_effects=True,
                                             vmem_limit_bytes=42 * 1024 * 1024),
    )(readings, channel_start.T, time_start.T)
    return outliers, left.T, right.T


def solution(mesh):
    n, m = mesh.shape["tm"], mesh.shape["chan"]
    specs = (P("chan", "tm"), P(("chan", "tm"), None), P(("tm", "chan"), None))
    return jax.shard_map(functools.partial(shards, n, m), mesh=mesh, in_specs=specs, out_specs=specs,
                         check_vma=False)
```
